32 devices in a mesh: seq: 8 (over z, y), head: 4 (over x, core).
Axes of the slice: x: 2, y: 2, z: 4, core: 2. Of those that a mesh axis runs over, the one named last changes fastest.
Arguments:
- queries: bfloat16 [2048, 2048], P('seq', 'head'), may hold values from -6 to 6
- keys: bfloat16 [2048, 2048], P('seq', 'head'), may hold values from -40 to 40
- values: bfloat16 [2048, 2048], P('seq', 'head'), may hold values from -24 to 24
- ridges: float32 [16], P('head'), may hold values from 0.25 to 4
- out_weight: bfloat16 [2048, 2048], P('head'), may hold values from -0.125 to 0.125
Outputs:
- layer_out: bfloat16 [2048, 2048], P('seq', 'head')
The draws below stay inside these ranges and needn't reach their ends.
All inputs are finite; a program needn't handle non-finite values.
Results may differ from the reference program's by a relative error of at most 0.0049.
Values may be sent and summed in bfloat16 or wider, within the bound.
A program may use at most 128 MiB of HBM per device.

```python
import math
import jax
import jax.numpy as jnp
from jax import lax

D = 2048
HEADS = 16
HD = 128
SPAN = 128
ITERS = 2
TOKENS = 2048


def draw_keys(key, part):
    first, second = jax.random.split(key, 2)
    scales = jnp.exp(jax.random.uniform(first, (1, HEADS * HD), jnp.float32, 0.0, math.log(10.0)))
    base = jax.random.normal(second, (TOKENS, HEADS * HD), jnp.float32) * scales
    return jnp.clip(base, -40.0, 40.0).astype(jnp.bfloat16)


def levels(own_key, dims, pieces, smallest, largest):
    loudness, own = 1.0, jax.random.fold_in(own_key, 6)
    for axis_at, shards_of in pieces:
        steps = jnp.exp(jax.random.uniform(jax.random.fold_in(own, axis_at), (shards_of,), jnp.float32, smallest / len(pieces), largest / len(pieces)))
        loudness = loudness * jnp.repeat(steps, dims[axis_at] // shards_of).reshape([-1 if axis == axis_at else 1 for axis in range(len(dims))])
    return loudness


def noise(stream_key, dims, width, most, cuts=(), held_as=jnp.bfloat16):
    level = levels(stream_key, dims, cuts, -0.22, 0.18) if cuts else 1.0
    values = jax.random.normal(stream_key, dims, jnp.float32) * width * level
    return jnp.minimum(jnp.maximum(values, -most), most).astype(held_as)


def setup_inputs(seed: int = 0) -> dict:
    arg_keys = jax.random.split(jax.random.key(seed), 6)
    queries = noise(arg_keys[0], (TOKENS, HEADS * HD), 1.0, 6.0, ((0, 8), (1, 4)))
    keys = draw_keys(jax.random.fold_in(arg_keys[5], 71), 0)
    values = noise(arg_keys[2], (TOKENS, HEADS * HD), 4.0, 24.0, ((0, 8), (1, 4)))
    ridges = jnp.clip(jnp.exp(math.log(4.0) - 2.7725887 * jax.random.uniform(arg_keys[3], (HEADS,), jnp.float32) ** levels(arg_keys[3], (HEADS,), ((0, 4),), -0.2, 0.2)), 0.25, 4.0)
    out_weight = noise(arg_keys[4], (HEADS * HD, D), (HEADS * HD) ** -0.5, 0.125, ((0, 4),))
    return dict(queries=queries, keys=keys, values=values, ridges=ridges, out_weight=out_weight)


highest = lax.Precision.HIGHEST

def normalize(entries):
    return entries * lax.rsqrt(lax.optimization_barrier(jnp.sum(entries * entries, axis=-1, keepdims=True)) + 1e-06)

def product(left, right):
    return jnp.dot(left, right, precision=highest, preferred_element_type=jnp.float32)

def solve_block(queries_b, keyrows, values_b, key_state, value_state, ridge_value):
    block_len = queries_b.shape[0]
    causal = (lax.broadcasted_iota(jnp.int32, (block_len, block_len), 0) >= lax.broadcasted_iota(jnp.int32, (block_len, block_len), 1)).astype(jnp.float32)

    def within(inputs, payload):
        scores = product(inputs, keyrows.T) * causal
        return product(scores, payload)

    def operate(direction):
        return ridge_value * direction + within(direction, keyrows) + product(direction, key_state)
    estimate = jnp.zeros_like(queries_b)
    residual = queries_b
    direction = queries_b
    res_norm = lax.optimization_barrier(jnp.sum(residual * residual, axis=-1, keepdims=True))
    for sweep in range(ITERS):
        applied = operate(direction)
        step_size = res_norm / (lax.optimization_barrier(jnp.sum(direction * applied, axis=-1, keepdims=True)) + 1e-06)
        estimate = estimate + step_size * direction
        residual = residual - step_size * applied
        fresh = lax.optimization_barrier(jnp.sum(residual * residual, axis=-1, keepdims=True))
        direction = residual + fresh / (res_norm + 1e-06) * direction
        res_norm = fresh
    return product(estimate, value_state) + within(estimate, values_b)

def one_head(operands):
    head_q, head_k, head_v, ridge_value = operands
    blocks_q = normalize(head_q).reshape(-1, SPAN, HD)
    blocks_k = normalize(head_k).reshape(-1, SPAN, HD)
    blocks_v = head_v.reshape(-1, SPAN, HD)

    def advance(carry, block):
        key_state, value_state = carry
        block_q, block_k, block_v = block
        result = solve_block(block_q, block_k, block_v, key_state, value_state, ridge_value)
        key_state = key_state + product(block_k.T, block_k)
        value_state = value_state + product(block_k.T, block_v)
        return ((key_state, value_state), result)
    start = (jnp.zeros((HD, HD), jnp.float32), jnp.zeros((HD, HD), jnp.float32))
    unused, results = lax.scan(advance, start, (blocks_q, blocks_k, blocks_v))
    return results.reshape(TOKENS, HD)

def reference(queries, keys, values, ridges, out_weight):
    split_q = queries.astype(jnp.float32).reshape(TOKENS, HEADS, HD).transpose(1, 0, 2)
    split_k = keys.astype(jnp.float32).reshape(TOKENS, HEADS, HD).transpose(1, 0, 2)
    split_v = values.astype(jnp.float32).reshape(TOKENS, HEADS, HD).transpose(1, 0, 2)
    outputs = lax.map(one_head, (split_q, split_k, split_v, ridges.astype(jnp.float32)))
    mixed = outputs.transpose(1, 0, 2).reshape(TOKENS, HEADS * HD).astype(jnp.bfloat16)
    return jnp.dot(mixed, out_weight, preferred_element_type=jnp.float32).astype(jnp.bfloat16)
```

```python
import functools

import jax
import jax.numpy as jnp
from jax import lax
from jax.experimental import pallas as pl
from jax.experimental.pallas import tpu as pltpu
from jax.sharding import PartitionSpec as P

MESH = pl.DeviceIdType.MESH
EPS = 1e-06


def split(value):
    high = value.astype(jnp.bfloat16)
    return high, (value - high.astype(jnp.float32)).astype(jnp.bfloat16)


def product(left, right, dims=((1,), (0,))):
    return lax.dot_general(left, right, (dims, ((), ())), preferred_element_type=jnp.float32)


def row_sum(value):
    return jnp.sum(value, axis=-1, keepdims=True)


def kernel(
    seqs, groups, heads,
    q_any, k_any, v_any, ridge_any, w_any, out_ref,
    ridge_ref, q_ref, k_ref, v_ref, weight,
    high_ref, low_ref, sums, sums_out, sums_in, run_out, run_in, past_out, past_in,
    qn_ref, first, mixed, total_ref,
    load_sem, w_sem, ws_sem, wr_sem, cs_sem, cr_sem, fs_sem, fr_sem,
    ss_sem, sr_sem, xs_sem, xr_sem, rs_sem, rr_sem, as_sem, ar_sem,
    ms_sem, mr_sem, ps_sem, pr_sem, gs_sem, gr_sem,
):
    seq, group = lax.axis_index("seq"), lax.axis_index("head")
    rank, side = seq // 2, seq % 2
    pair, lane = group // 2, group % 2
    ranks, pairs = seqs // 2, groups // 2
    tokens, width = out_ref.shape
    hd = q_ref.shape[1] // heads
    twin_seq, twin_head = seq + 1 - 2 * side, group + 1 - 2 * lane
    not_first, not_last = rank > 0, rank < ranks - 1

    loads = [
        pltpu.make_async_copy(src, dst, load_sem.at[at])
        for at, (src, dst) in enumerate(
            ((k_any, k_ref), (v_any, v_ref), (q_any, q_ref), (ridge_any, ridge_ref))
        )
    ]
    for load in loads:
        load.start()

    def columns(at, parity):
        return pl.ds(pl.multiple_of((2 * at + parity) * width, 128), width)

    w_load = pltpu.make_async_copy(w_any.at[:, columns(pair, lane)], weight.at[0], w_sem)
    w_load.start()

    barrier = pltpu.get_barrier_semaphore()

    def greet(**device):
        pl.semaphore_signal(barrier, inc=1, device_id=device, device_id_type=MESH)

    greet(seq=twin_seq)
    greet(head=twin_head)
    for off in range(1, pairs):
        for parity in range(2):
            greet(head=2 * ((pair + off) % pairs) + parity)

    @pl.when(not_first)
    def _():
        greet(seq=seq - 2)

    @pl.when(not_last)
    def _():
        greet(seq=seq + 2)

    w_send = pltpu.make_async_remote_copy(
        w_any.at[:, columns(pair, 1 - lane)], weight.at[1], ws_sem, wr_sem,
        device_id={"head": twin_head}, device_id_type=MESH,
    )
    shares = 2 if ranks % 2 == 0 else 1
    parts = 2
    part = hd // parts
    blocks = parts * heads // shares
    turn = rank % shares
    cross_sends, relays = [], []
    for block in range(blocks):
        for flip in range(2):
            for off in range(1, pairs):
                target = (pair + off) % pairs
                parity = lane if flip == 0 else 1 - lane
                slot = 2 * (pairs - off) + flip
                row = pl.ds(pl.multiple_of((turn * blocks + block) * part, part), part)
                index = (slot - 2) * blocks + block
                cross_sends.append(
                    pltpu.make_async_remote_copy(
                        w_any.at[row, columns(target, parity)], weight.at[slot, row],
                        cs_sem.at[index], cr_sem.at[index],
                        device_id={"head": 2 * target + parity}, device_id_type=MESH,
                    )
                )
                relays.append(
                    pltpu.make_async_remote_copy(
                        weight.at[slot, row], weight.at[slot, row],
                        fs_sem.at[index], fr_sem.at[index],
                        device_id={"seq": seq + 2 - 4 * (rank % 2)}, device_id_type=MESH,
                    )
                )

    def relay(index):
        cross_sends[index].wait_recv()
        if shares == 2:
            relays[index].start()

    pl.semaphore_wait(barrier, 2 * pairs + not_first.astype(jnp.int32) + not_last.astype(jnp.int32))
    for send in cross_sends:
        send.start()
    w_send.start()

    loads[0].wait()
    loads[1].wait()
    near, far = side, 1 - side
    sum_sends, extra_sends = [], []
    for at in range(heads):
        span = slice(at * hd, (at + 1) * hd)
        keys = k_ref[:, span].astype(jnp.float32)
        scale = lax.rsqrt(row_sum(keys * keys) + EPS)
        payload = jnp.concatenate(
            [keys * (scale * scale), v_ref[:, span].astype(jnp.float32) * scale], axis=1
        )
        high, low = split(payload)
        high_ref[at] = high
        low_ref[at] = low
        both = ((0,), (0,))
        total = product(k_ref[:, span], high, both) + product(k_ref[:, span], low, both)
        sums[0, at] = total[:, :hd]
        sums[1, at] = total[:, hd:]
        sums_out[0, at] = total[:, :hd].astype(jnp.bfloat16)
        sums_out[1, at] = total[:, hd:].astype(jnp.bfloat16)
        send = pltpu.make_async_remote_copy(
            sums_out.at[far, at], sums_in.at[far, at], ss_sem.at[at], sr_sem.at[at],
            device_id={"seq": twin_seq}, device_id_type=MESH,
        )
        send.start()
        sum_sends.append(send)
        extra_sends.append(
            pltpu.make_async_remote_copy(
                sums_out.at[0, at], sums_in.at[0, at], xs_sem.at[at], xr_sem.at[at],
                device_id={"seq": twin_seq}, device_id_type=MESH,
            )
        )

    @pl.when(side == 0)
    def _():
        for send in extra_sends:
            send.start()


    causal = lax.broadcasted_iota(jnp.int32, (tokens, tokens), 0) >= lax.broadcasted_iota(
        jnp.int32, (tokens, tokens), 1
    )

    def within(at, parts):
        keys = k_ref[:, at * hd:(at + 1) * hd]
        across = ((1,), (1,))
        scores = product(parts[0], keys, across) + product(parts[1], keys, across)
        high, low = split(jnp.where(causal, scores, 0.0))
        payload = high_ref[at]
        return product(high, payload) + product(low, payload) + product(high, low_ref[at])

    bits = run_out.shape[1]
    bit = hd // bits
    run_sends = [
        [
            pltpu.make_async_remote_copy(
                run_out.at[at, piece], run_in.at[at, piece],
                rs_sem.at[at, piece], rr_sem.at[at, piece],
                device_id={"seq": (seq + 2) % seqs}, device_id_type=MESH,
            )
            for piece in range(bits)
        ]
        for at in range(heads)
    ]
    past_sends = [
        [
            pltpu.make_async_remote_copy(
                past_out.at[at, piece], past_in.at[at, piece],
                as_sem.at[at, piece], ar_sem.at[at, piece],
                device_id={"seq": twin_seq}, device_id_type=MESH,
            )
            for piece in range(bits)
        ]
        for at in range(heads)
    ]

    def gathered(at):
        sum_sends[at].wait_recv()
        sums[near, at] += sums_in[near, at].astype(jnp.float32)

    @pl.when(rank == 0)
    def _():
        past_out[...] = jnp.zeros(past_out.shape, past_out.dtype)
        past_in[...] = jnp.zeros(past_in.shape, past_in.dtype)
        for at in range(heads):
            gathered(at)

            @pl.when(not_last)
            def _():
                for piece in range(bits):
                    span = slice(piece * bit, (piece + 1) * bit)
                    run_out[at, piece] = sums[near, at, span].astype(run_out.dtype)
                    run_sends[at][piece].start()

    loads[2].wait()
    loads[3].wait()
    for at in range(heads):
        q = q_ref[:, at * hd:(at + 1) * hd].astype(jnp.float32)
        q = q * lax.rsqrt(row_sum(q * q) + EPS)
        qn_ref[at] = q
        first[at] = within(at, split(q))

    behind = len(relays) - 2
    for index in range(behind):

        @pl.when(index < rank)
        def _():
            relay(index)

    @pl.when(not_first)
    def _():
        for at in range(heads):
            gathered(at)
        for at in range(heads):
            for piece in range(bits):
                span = slice(piece * bit, (piece + 1) * bit)
                run_sends[at][piece].wait_recv()
                past_out[at, piece] = run_in[at, piece].astype(past_out.dtype)
                past_sends[at][piece].start()

                @pl.when(not_last)
                def _():
                    run_out[at, piece] = (
                        run_in[at, piece].astype(jnp.float32) + sums[near, at, span]
                    ).astype(run_out.dtype)
                    run_sends[at][piece].start()

    @pl.when(side == 1)
    def _():
        for send in extra_sends:
            send.wait_recv()

    for index in range(behind):

        @pl.when(index >= rank)
        def _():
            relay(index)

    mixed_sends, cross_mixed, relay_mixed = [], [], []

    def solve(at):
        @pl.when(not_first)
        def _():
            for piece in range(bits):
                past_sends[at][piece].wait_recv()

        given, held = past_in[at].reshape(hd, hd), past_out[at].reshape(hd, hd)
        left = side == 0
        none = jnp.zeros((hd, hd), jnp.bfloat16)
        state = jnp.concatenate(
            [
                jnp.concatenate([jnp.where(left, held, given), jnp.where(left, given, held)], axis=1),
                jnp.concatenate(
                    [jnp.where(left, none, sums_in[0, at]), jnp.where(left, none, sums_in[1, at])], axis=1
                ),
            ],
            axis=0,
        )

        def carried(parts):
            high, low = parts
            return product(jnp.concatenate([high, high], axis=1), state) + product(
                jnp.concatenate([low, low], axis=1), state
            )

        ridge = ridge_ref[at]
        q = qn_ref[at]
        whole = first[at] + carried(split(q))
        norm = row_sum(q * q)
        applied = whole[:, :hd] + ridge * q
        step = norm / (row_sum(q * applied) + EPS)
        residual = q - step * applied
        fresh = row_sum(residual * residual)
        direction = residual + fresh / (norm + EPS) * q
        parts = split(direction)
        again = within(at, parts) + carried(parts)
        applied = again[:, :hd] + ridge * direction
        after = fresh / (row_sum(direction * applied) + EPS)
        span = slice(at * hd, (at + 1) * hd)
        mixed[0, :, span] = (step * whole[:, hd:] + after * again[:, hd:]).astype(jnp.bfloat16)
        for off in range(1, pairs):
            target, slot = (pair + off) % pairs, 2 * (pairs - off)
            index = (pairs - off - 1) * heads + at
            send = pltpu.make_async_remote_copy(
                mixed.at[0, :, span], mixed.at[slot, :, span], ps_sem.at[index], pr_sem.at[index],
                device_id={"head": 2 * target + lane}, device_id_type=MESH,
            )
            send.start()
            cross_mixed.append(send)
            relay_mixed.append(
                pltpu.make_async_remote_copy(
                    mixed.at[slot, :, span], mixed.at[slot + 1, :, span],
                    gs_sem.at[index], gr_sem.at[index],
                    device_id={"head": twin_head}, device_id_type=MESH,
                )
            )
        send = pltpu.make_async_remote_copy(
            mixed.at[0, :, span], mixed.at[1, :, span], ms_sem.at[at], mr_sem.at[at],
            device_id={"head": twin_head}, device_id_type=MESH,
        )
        send.start()
        mixed_sends.append(send)

    for at in range(heads):
        solve(at)
        if at < 2:
            relay(behind + at)

    def pass_on(at):
        for index in range(at * (pairs - 1), (at + 1) * (pairs - 1)):
            cross_mixed[index].wait_recv()
            relay_mixed[index].start()

    pass_on(0)
    w_load.wait()
    total_ref[...] = product(mixed[0], weight[0])
    pass_on(1)
    w_send.wait_recv()
    for send in mixed_sends:
        send.wait_recv()
    total_ref[...] += product(mixed[1], weight[1])
    for at in range(2, heads):
        pass_on(at)
    if shares == 2:
        for send in relays:
            send.wait_recv()
    most = (heads - 1) * hd
    early, late = relay_mixed[:(heads - 1) * (pairs - 1)], relay_mixed[(heads - 1) * (pairs - 1):]
    for slot in range(2, 2 * pairs, 2):
        total_ref[...] += product(mixed[slot], weight[slot])
    for send in early:
        send.wait_recv()
    for slot in range(3, 2 * pairs, 2):
        total_ref[...] += product(mixed[slot, :, :most], weight[slot, :most, :])
    for send in late:
        send.wait_recv()
    total = total_ref[...]
    for slot in range(3, 2 * pairs, 2):
        total = total + product(mixed[slot, :, most:], weight[slot, most:, :])
    out_ref[...] = total.astype(out_ref.dtype)

    for send in sum_sends + [w_send] + cross_sends + mixed_sends + cross_mixed + relay_mixed:
        send.wait_send()
    if shares == 2:
        for send in relays:
            send.wait_send()

    @pl.when(side == 0)
    def _():
        for send in extra_sends:
            send.wait_send()

    @pl.when(not_first)
    def _():
        for send in sum(past_sends, []):
            send.wait_send()

    @pl.when(not_last)
    def _():
        for send in sum(run_sends, []):
            send.wait_send()


def solution(mesh):
    seqs, groups = mesh.shape["seq"], mesh.shape["head"]

    def shards(queries, keys, values, ridges, out_weight):
        tokens, wide = queries.shape
        heads = ridges.shape[0]
        hd = wide // heads
        rows, model = out_weight.shape
        width = model // groups
        pairs = groups // 2
        bits = 2
        crossing = max(4 * (pairs - 1) * (heads // (2 if (seqs // 2) % 2 == 0 else 1)), 1)
        others = max((pairs - 1) * heads, 1)
        bf16, f32 = jnp.bfloat16, jnp.float32
        wire = bf16 if seqs <= 8 else f32
        near_by = [pltpu.with_memory_space_constraint(each, pltpu.HBM) for each in (queries, keys, values, ridges, out_weight)]
        dma = pltpu.SemaphoreType.DMA
        any_spec = pl.BlockSpec(memory_space=pl.ANY)
        return pl.pallas_call(
            functools.partial(kernel, seqs, groups, heads),
            out_shape=jax.ShapeDtypeStruct((tokens, width), bf16),
            in_specs=[any_spec] * 5,
            out_specs=pl.BlockSpec(memory_space=pltpu.VMEM),
            scratch_shapes=[
                pltpu.SMEM((heads,), f32),
                pltpu.VMEM((tokens, wide), bf16),
                pltpu.VMEM((tokens, wide), bf16),
                pltpu.VMEM((tokens, wide), bf16),
                pltpu.VMEM((groups, rows, width), bf16),
                pltpu.VMEM((heads, tokens, 2 * hd), bf16),
                pltpu.VMEM((heads, tokens, 2 * hd), bf16),
                pltpu.VMEM((2, heads, hd, hd), f32),
                pltpu.VMEM((2, heads, hd, hd), bf16),
                pltpu.VMEM((2, heads, hd, hd), bf16),
                pltpu.VMEM((heads, bits, hd // bits, hd), wire),
                pltpu.VMEM((heads, bits, hd // bits, hd), wire),
                pltpu.VMEM((heads, bits, hd // bits, hd), bf16),
                pltpu.VMEM((heads, bits, hd // bits, hd), bf16),
                pltpu.VMEM((heads, tokens, hd), f32),
                pltpu.VMEM((heads, tokens, 2 * hd), f32),
                pltpu.VMEM((groups, tokens, wide), bf16),
                pltpu.VMEM((tokens, width), f32),
                dma((4,)), dma, dma, dma,
                dma((crossing,)), dma((crossing,)), dma((crossing,)), dma((crossing,)),
                dma((heads,)), dma((heads,)), dma((heads,)), dma((heads,)),
                dma((heads, bits)), dma((heads, bits)), dma((heads, bits)), dma((heads, bits)),
                dma((heads,)), dma((heads,)), dma((others,)), dma((others,)), dma((others,)), dma((others,)),
            ],
            compiler_params=pltpu.CompilerParams(
                collective_id=0, has_side_effects=True, vmem_limit_bytes=24 * 2**20
            ),
        )(*near_by)

    in_specs = (P("seq", "head"), P("seq", "head"), P("seq", "head"), P("head"), P("head", None))
    return jax.shard_map(
        shards, mesh=mesh, in_specs=in_specs, out_specs=P("seq", "head"), check_vma=False
    )
```
